256 devices in a mesh: dp: 8 (over y, z_hi), latent: 32 (over z_lo, x, core).
Axes of the slice: x: 4, y: 4, z: 8 (z_hi: 2, z_lo: 4; z = z_hi * 4 + z_lo), core: 2. Of those that a mesh axis runs over, the one named last changes fastest.
Arguments:
- resid: bfloat16 [512, 4608], P('dp'), may hold values from -24 to 24
- enc_weight: bfloat16 [4608, 131072], P(None, ('dp', 'latent')), may hold values from -0.09375 to 0.09375
- enc_bias: float32 [131072], P(('dp', 'latent')), may hold values from -3 to 3
- thresholds: float32 [131072], P(('dp', 'latent')), may hold values from 0.5 to 3
- dec_weight: bfloat16 [131072, 4608], P(('dp', 'latent')), may hold values from -0.09375 to 0.09375
- dec_bias: float32 [4608], replicated, may hold values from -7 to 7
- refusal_ids: int32 [16], replicated, may hold values from 0 to 131071, as said below
- clamp_levels: int32 [16], replicated, may hold values from 1 to 8
Outputs:
- steered: bfloat16 [512, 4608], P('dp')
The draws below stay inside these ranges and needn't reach their ends.
Inputs may be any that keep to these rules, and one draw needn't show every extreme that they name: `refusal_ids`: an index may be named more than once, with different clamp levels.
All inputs are finite; a program needn't handle non-finite values.
Results may differ from the reference program's by a relative error of at most 0.0052.
Values may be sent and summed in bfloat16 or wider, within the bound.
No kernel may reach another device: no remote copies, remote signals or barrier semaphores. Data moves between devices by JAX's collectives and lax.ppermute only.
A program may use at most 128 MiB of HBM per device.

```python
import math
import jax
import jax.numpy as jnp
from jax import lax

D = 4608
LATENTS = 131072
K = 16
TOKENS = 512


def scales_of(key, length, low, high, wobble):
    log_ramp = jnp.linspace(math.log(low), math.log(high), length)
    return jnp.exp(log_ramp + jax.random.uniform(key, (length,), jnp.float32, -wobble, wobble))


def draw_resid(key, part):
    k_base, k_rows, k_cols = jax.random.split(key, 3)
    values = jnp.clip(jax.random.normal(k_base, (TOKENS, D), jnp.float32), -4.0, 4.0)
    row_scale = jnp.exp(jax.random.uniform(k_rows, (TOKENS, 1), jnp.float32, math.log(0.3), math.log(3.0)))
    col_scale = scales_of(k_cols, D, 0.4, 1.2, 0.5)
    return (values * row_scale * col_scale[None, :]).astype(jnp.bfloat16)


def draw_dec_bias(key, part):
    k_base, k_cols = jax.random.split(key, 2)
    values = jnp.clip(jax.random.normal(k_base, (D,), jnp.float32), -4.0, 4.0)
    return values * scales_of(k_cols, D, 0.3, 1.0, 0.5)


def refusal_table(key):
    k_ids, k_src, k_first, k_up, k_down, k_rest = jax.random.split(jax.random.fold_in(key, 31), 6)
    half_count = K // 2
    quarter_count = K // 4
    id_values = jax.random.randint(k_ids, (K,), 0, LATENTS, dtype=jnp.int32)
    source_slots = jax.random.permutation(k_src, half_count)[:quarter_count].astype(jnp.int32)
    copy_slots = half_count + jnp.arange(quarter_count, dtype=jnp.int32)
    id_values = id_values.at[copy_slots].set(id_values[source_slots])
    id_values = id_values.at[K - 2].set(0).at[K - 1].set(LATENTS - 1)
    level_values = jax.random.randint(k_rest, (K,), 1, 9, dtype=jnp.int32)
    first_levels = jax.random.randint(k_first, (half_count,), 3, 7, dtype=jnp.int32)
    level_values = level_values.at[:half_count].set(first_levels)
    source_levels = first_levels[source_slots]
    raised = jax.random.randint(k_up, (quarter_count,), source_levels + 2, 9, dtype=jnp.int32)
    lowered = jax.random.randint(k_down, (quarter_count,), 1, source_levels - 1, dtype=jnp.int32)
    raise_mask = jnp.arange(quarter_count, dtype=jnp.int32) % 2 == 0
    level_values = level_values.at[copy_slots].set(jnp.where(raise_mask, raised, lowered))
    level_values = level_values.at[K - 2].set(1).at[K - 1].set(8)
    return (id_values, level_values)


def draw_refusal_ids(key, part):
    return refusal_table(key)[0]


def draw_clamp_levels(key, part):
    return refusal_table(key)[1]


def block_levels(own_key, extent, cuts, low, high):
    factor_of = 1.0
    for position, blocks in cuts:
        draws = jax.random.uniform(jax.random.fold_in(jax.random.fold_in(own_key, 6), position), (blocks,), jnp.float32, low / len(cuts), high / len(cuts))
        factor_of = factor_of * jnp.repeat(jnp.exp(draws), extent[position] // blocks).reshape((-1,) + (1,) * (len(extent) - 1 - position))
    return factor_of


def bell_draw(own_key, dims, spread, most, pieces=(), held_as=jnp.bfloat16):
    array = jax.random.normal(own_key, dims, jnp.float32) * spread
    if len(pieces) > 0:
        array = block_levels(own_key, dims, pieces, -0.22, 0.18) * array
    return jnp.clip(array, min=-most, max=most).astype(held_as)


def setup_inputs(seed: int = 0) -> dict:
    keys = jax.random.split(jax.random.key(seed), 9)
    return {
        "resid": draw_resid(jax.random.fold_in(keys[8], 71), 0),
        "enc_weight": bell_draw(keys[1], (D, LATENTS), D ** -0.5, 0.09375, ((1, 256),)),
        "enc_bias": bell_draw(keys[2], (LATENTS,), 0.5, 3.0, ((0, 256),), jnp.float32),
        "thresholds": jnp.clip(jnp.exp(math.log(3.0) - 1.7917595 * jax.random.uniform(keys[3], (LATENTS,), jnp.float32) ** block_levels(keys[3], (LATENTS,), ((0, 256),), -0.2, 0.2)), 0.5, 3.0),
        "dec_weight": bell_draw(keys[4], (LATENTS, D), D ** -0.5, 0.09375, ((0, 256),)),
        "dec_bias": draw_dec_bias(jax.random.fold_in(keys[8], 71), 0),
        "refusal_ids": draw_refusal_ids(jax.random.fold_in(keys[8], 71), 0),
        "clamp_levels": draw_clamp_levels(jax.random.fold_in(keys[8], 71), 0),
    }


gate_width = 0.1
norm_eps = 1e-06

def gate_latents(pre_acts, thresh_part):
    return pre_acts * jax.nn.sigmoid((pre_acts - thresh_part) / gate_width)

def clamp_block(activations, columns, refusal_ids, clamp_levels, thresh_part):
    matched = refusal_ids[:, None] == columns[None, :]
    targets_all = clamp_levels.astype(jnp.float32)[:, None] * thresh_part[None, :]
    targets = lax.optimization_barrier(jnp.max(jnp.where(matched, targets_all, -1.0), axis=0))
    is_named = jnp.any(matched, axis=0)
    return jnp.where(is_named[None, :], jnp.maximum(activations, targets[None, :]), activations)

def reference(resid, enc_weight, enc_bias, thresholds, dec_weight, dec_bias, refusal_ids, clamp_levels):
    block_count = 16
    block_width = LATENTS // block_count

    def one_block(running, block_index):
        offset = block_index * block_width
        w_enc = lax.dynamic_slice_in_dim(enc_weight, offset, block_width, 1)
        w_dec = lax.dynamic_slice_in_dim(dec_weight, offset, block_width, 0)
        bias_part = lax.dynamic_slice_in_dim(enc_bias, offset, block_width, 0)
        thresh_part = lax.dynamic_slice_in_dim(thresholds, offset, block_width, 0)
        pre_acts = jnp.dot(resid, w_enc, preferred_element_type=jnp.float32) + bias_part
        columns = offset + jnp.arange(block_width, dtype=jnp.int32)
        clamped = clamp_block(gate_latents(pre_acts, thresh_part), columns, refusal_ids, clamp_levels, thresh_part).astype(jnp.bfloat16)
        return (running + jnp.dot(clamped, w_dec, preferred_element_type=jnp.float32), None)
    recon, _ = lax.scan(one_block, jnp.zeros((TOKENS, D), jnp.float32), jnp.arange(block_count, dtype=jnp.int32))
    recon = recon + dec_bias
    in_sq = lax.optimization_barrier(jnp.sum(jnp.square(resid.astype(jnp.float32)), axis=1, keepdims=True))
    out_sq = lax.optimization_barrier(jnp.sum(jnp.square(recon), axis=1, keepdims=True))
    return (recon * jnp.sqrt((in_sq + norm_eps) / (out_sq + norm_eps))).astype(jnp.bfloat16)
```

```python
import jax
import jax.numpy as jnp
from jax import lax
from jax.sharding import PartitionSpec as P

gate_width = 0.1
norm_eps = 1e-06
AXES = ("dp", "latent")


def pairs_of(move):
    out = []
    for y in range(4):
        for zh in range(2):
            for zl in range(4):
                for x in range(4):
                    for c in range(2):
                        t = move(y, zh, zl, x, c)
                        src = (((y * 2 + zh) * 4 + zl) * 4 + x) * 2 + c
                        dst = (((t[0] * 2 + t[1]) * 4 + t[2]) * 4 + t[3]) * 2 + t[4]
                        out.append((src, dst))
    return out


def send(v, move):
    return lax.ppermute(v, AXES, pairs_of(move))


def to_bulk(k):
    return lambda y, zh, zl, x, c: (y, zh, zl, (x + k) % 4, c) if c == 0 else ((y + k) % 4, zh, zl, x, c)


def to_side(k):
    return lambda y, zh, zl, x, c: ((y + k) % 4, zh, zl, x, c) if c == 0 else (y, zh, zl, (x + k) % 4, c)


def to_x(k):
    return lambda y, zh, zl, x, c: (y, zh, zl, (x + k) % 4, c)


def to_mirror(y, zh, zl, x, c):
    return (y, 1 - zh, 3 - zl, x, c)


def to_zl(bit):
    return lambda y, zh, zl, x, c: (y, zh, zl ^ bit, x, c)


def to_core(y, zh, zl, x, c):
    return (y, zh, zl, x, 1 - c)


def gate_latents(pre_acts, thresh_part):
    return pre_acts * jax.nn.sigmoid((pre_acts - thresh_part) / gate_width)


def clamp_targets(columns, refusal_ids, clamp_levels, thresh_part):
    matched = refusal_ids[:, None] == columns[None, :]
    targets_all = clamp_levels.astype(jnp.float32)[:, None] * thresh_part[None, :]
    targets = jnp.max(jnp.where(matched, targets_all, -1.0), axis=0)
    return jnp.where(jnp.any(matched, axis=0), targets, -jnp.inf)


def body(resid, enc_weight, enc_bias, thresholds, dec_weight, dec_bias, refusal_ids, clamp_levels):
    bf16, f32 = jnp.bfloat16, jnp.float32
    hold = lax.optimization_barrier
    lat_dev = enc_weight.shape[1]
    width = resid.shape[1]
    dp_index = lax.axis_index("dp")
    lat_index = lax.axis_index("latent")
    x_index = (lat_index // 2) % 4
    core = lat_index % 2
    own = lax.dynamic_slice_in_dim(resid, x_index * 16 + core * 8, 8, 0)

    other = send(own, to_mirror)
    rows1 = jnp.stack([own, other])
    rows1, enc_weight, dec_weight = hold((rows1, enc_weight, dec_weight))
    rows2 = jnp.stack([rows1] + [send(rows1, to_side(-k)) for k in (1, 2, 3)])
    rows2 = hold(rows2.reshape(64, width))
    rows3 = [rows2] + [send(rows2, to_bulk(-k)) for k in (1, 2, 3)]
    rows = jnp.concatenate(rows3, axis=0)

    enc_other = send(enc_weight, to_core)
    dec_other = send(dec_weight, to_core)
    small_other = send(jnp.stack([enc_bias, thresholds]), to_core)
    base = (dp_index * 32 + lat_index) * lat_dev
    base_other = (dp_index * 32 + lat_index + 1 - 2 * core) * lat_dev
    iota = jnp.arange(lat_dev, dtype=jnp.int32)

    def encode(weight, bias, thr, first):
        targets = clamp_targets(first + iota, refusal_ids, clamp_levels, thr)
        pre_acts = jnp.dot(rows, weight, preferred_element_type=f32) + bias
        return jnp.maximum(gate_latents(pre_acts, thr), targets[None, :]).astype(bf16)

    acts = encode(enc_weight, enc_bias, thresholds, base)
    acts_other = encode(enc_other, small_other[0], small_other[1], base_other)
    part = jnp.dot(acts, dec_weight, preferred_element_type=f32) + jnp.dot(
        acts_other, dec_other, preferred_element_type=f32
    )
    part = part.reshape(4, 64, width)

    sum1 = part[0]
    for k in (2, 1, 3):
        sum1 = sum1 + send(part[k].astype(bf16), to_bulk(k)).astype(f32)
    sum1 = sum1.reshape(4, 16, width)
    sum2 = sum1[0]
    for k in (2, 1, 3):
        sum2 = sum2 + send(sum1[k].astype(bf16), to_side(k)).astype(f32)
    sum2 = sum2.reshape(2, 8, width)
    sum3 = sum2[0] + send(sum2[1].astype(bf16), to_mirror).astype(f32)
    mine = hold(sum3.astype(bf16))
    sum4 = mine.astype(f32) + send(mine, to_zl(1)).astype(f32)
    mine = hold(sum4.astype(bf16))
    recon = mine.astype(f32) + send(mine, to_zl(2)).astype(f32) + dec_bias

    in_sq = jnp.sum(jnp.square(own.astype(f32)), axis=1, keepdims=True)
    out_sq = jnp.sum(jnp.square(recon), axis=1, keepdims=True)
    scaled = hold((recon * jnp.sqrt((in_sq + norm_eps) / (out_sq + norm_eps))).astype(bf16))

    groups = jnp.stack([scaled] + [send(scaled, to_x(-k)) for k in (1, 2, 3)])
    groups = hold(groups)
    groups_other = send(groups, to_core)
    first = jnp.where(core == 0, groups, groups_other)
    second = jnp.where(core == 0, groups_other, groups)
    both = jnp.stack([first, second], axis=1).reshape(64, width)
    twice = jnp.concatenate([both, both], axis=0)
    return lax.dynamic_slice_in_dim(twice, (4 - x_index) % 4 * 16, 64, 0)


def solution(mesh):
    in_specs = (
        P("dp", None),
        P(None, ("dp", "latent")),
        P(("dp", "latent")),
        P(("dp", "latent")),
        P(("dp", "latent"), None),
        P(),
        P(),
        P(),
    )
    out_specs = P("dp", None)
    return jax.shard_map(body, mesh=mesh, in_specs=in_specs, out_specs=out_specs, check_vma=False)
```

```python
import jax
import jax.numpy as jnp
from jax import lax
from jax.experimental import pallas as pl
from jax.experimental.pallas import tpu as pltpu
from jax.sharding import PartitionSpec as P

gate_width = 0.1
norm_eps = 1e-06
AXES = ("dp", "latent")


def pairs_of(move):
    out = []
    for y in range(4):
        for zh in range(2):
            for zl in range(4):
                for x in range(4):
                    for c in range(2):
                        t = move(y, zh, zl, x, c)
                        src = (((y * 2 + zh) * 4 + zl) * 4 + x) * 2 + c
                        dst = (((t[0] * 2 + t[1]) * 4 + t[2]) * 4 + t[3]) * 2 + t[4]
                        out.append((src, dst))
    return out


def send(v, move):
    return lax.ppermute(v, AXES, pairs_of(move))


def to_bulk(k):
    return lambda y, zh, zl, x, c: (y, zh, zl, (x + k) % 4, c) if c == 0 else ((y + k) % 4, zh, zl, x, c)


def to_side(k):
    return lambda y, zh, zl, x, c: ((y + k) % 4, zh, zl, x, c) if c == 0 else (y, zh, zl, (x + k) % 4, c)


def to_x(k):
    return lambda y, zh, zl, x, c: (y, zh, zl, (x + k) % 4, c)


def to_mirror(y, zh, zl, x, c):
    return (y, 1 - zh, 3 - zl, x, c)


def to_zl(bit):
    return lambda y, zh, zl, x, c: (y, zh, zl ^ bit, x, c)


def to_core(y, zh, zl, x, c):
    return (y, zh, zl, x, 1 - c)


def gate_latents(pre_acts, thresh_part):
    return pre_acts * jax.nn.sigmoid((pre_acts - thresh_part) / gate_width)


def clamp_targets(columns, refusal_ids, clamp_levels, thresh_part):
    matched = refusal_ids[:, None] == columns[None, :]
    targets_all = clamp_levels.astype(jnp.float32)[:, None] * thresh_part[None, :]
    targets = jnp.max(jnp.where(matched, targets_all, -1.0), axis=0)
    return jnp.where(jnp.any(matched, axis=0), targets, -jnp.inf)


ENC_BLOCK = 256
DEC_BLOCK = 768
IN_FLIGHT = 4


def encode_block(rows, weight, aux_ref, acts_buf, b):
    lanes = pl.ds(b * ENC_BLOCK, ENC_BLOCK)
    bias, thr, floor = aux_ref[0:1, lanes], aux_ref[1:2, lanes], aux_ref[2:3, lanes]
    pre_acts = jnp.dot(rows, weight, preferred_element_type=jnp.float32) + bias
    acts_buf[:, lanes] = jnp.maximum(gate_latents(pre_acts, thr), floor).astype(jnp.bfloat16)


def first_kernel(rows_ref, aux_ref, enc_own, enc_other, dec_own, dec_other, enc_buf, dec_buf, part, acts_buf, sems):
    lat_dev = enc_own.shape[1]
    halves = lat_dev // ENC_BLOCK
    count = dec_own.shape[1] // DEC_BLOCK
    copies = []
    for b in range(2 * halves):
        src = enc_own if b < halves else enc_other
        lanes = pl.ds(b % halves * ENC_BLOCK, ENC_BLOCK)
        copies.append(pltpu.make_async_copy(src.at[:, lanes], enc_buf.at[b], sems.at[b]))
    for n in range(count):
        for h, src in enumerate((dec_own, dec_other)):
            lanes = pl.ds(n * DEC_BLOCK, DEC_BLOCK)
            rows = pl.ds(h * lat_dev, lat_dev)
            copies.append(pltpu.make_async_copy(src.at[:, lanes], dec_buf.at[n, rows], sems.at[len(copies)]))
    for copy in copies[:IN_FLIGHT]:
        copy.start()

    def arrive(i):
        copies[i].wait()
        if i + IN_FLIGHT < len(copies):
            copies[i + IN_FLIGHT].start()

    rows = rows_ref[...]
    for b in range(2 * halves):
        arrive(b)
        encode_block(rows, enc_buf[b], aux_ref, acts_buf, b)
    for n in range(count):
        arrive(2 * halves + 2 * n)
        arrive(2 * halves + 2 * n + 1)
        lanes = pl.ds(n * DEC_BLOCK, DEC_BLOCK)
        part[:, lanes] = jnp.dot(acts_buf[...], dec_buf[n], preferred_element_type=jnp.float32)


def rest_kernel(near1, near3, far, aux_ref, enc_buf, dec_buf, out1, out3, out2, acts_buf):
    rows = jnp.concatenate([near1[...], near3[...], far[...]], axis=0)
    size = near1.shape[0]
    for b in range(enc_buf.shape[0]):
        encode_block(rows, enc_buf[b], aux_ref, acts_buf, b)
    for n in range(dec_buf.shape[0]):
        lanes = pl.ds(n * DEC_BLOCK, DEC_BLOCK)
        part = jnp.dot(acts_buf[...], dec_buf[n], preferred_element_type=jnp.float32).astype(jnp.bfloat16)
        for p, out in enumerate((out1, out3, out2)):
            out[:, lanes] = part[p * size : (p + 1) * size]


def first_part(rows, aux, enc_own, enc_other, dec_own, dec_other):
    width, lat_dev = enc_own.shape
    vmem = pl.BlockSpec(memory_space=pltpu.VMEM)
    hbm = pl.BlockSpec(memory_space=pltpu.HBM)
    blocks, count = 2 * lat_dev // ENC_BLOCK, width // DEC_BLOCK
    total = rows.shape[0]
    return pl.pallas_call(
        first_kernel,
        out_shape=[
            pltpu.VMEM((blocks, width, ENC_BLOCK), jnp.bfloat16),
            pltpu.VMEM((count, 2 * lat_dev, DEC_BLOCK), jnp.bfloat16),
            pltpu.VMEM(rows.shape, jnp.float32),
        ],
        in_specs=[vmem] * 2 + [hbm] * 4,
        out_specs=[vmem] * 3,
        scratch_shapes=[
            pltpu.VMEM((total, 2 * lat_dev), jnp.bfloat16),
            pltpu.SemaphoreType.DMA((blocks + 2 * count,)),
        ],
        compiler_params=pltpu.CompilerParams(vmem_limit_bytes=VMEM_FIRST),
        cost_estimate=pl.CostEstimate(
            flops=8 * total * width * lat_dev, bytes_accessed=8 * width * lat_dev, transcendentals=2 * total * lat_dev
        ),
        name="first_part",
    )(rows, aux, enc_own, enc_other, dec_own, dec_other)


def rest_part(pieces, aux, enc_buf, dec_buf):
    vmem = pl.BlockSpec(memory_space=pltpu.VMEM)
    total = sum(p.shape[0] for p in pieces)
    blocks, width, _ = enc_buf.shape
    lat = blocks * ENC_BLOCK
    return pl.pallas_call(
        rest_kernel,
        out_shape=[pltpu.VMEM(p.shape, jnp.bfloat16) for p in pieces],
        in_specs=[vmem] * 6,
        out_specs=[vmem] * 3,
        scratch_shapes=[pltpu.VMEM((total, lat), jnp.bfloat16)],
        compiler_params=pltpu.CompilerParams(vmem_limit_bytes=VMEM_REST),
        cost_estimate=pl.CostEstimate(
            flops=4 * total * width * lat, bytes_accessed=4 * total * width, transcendentals=total * lat
        ),
        name="rest_part",
    )(*pieces, aux, enc_buf, dec_buf)


VMEM_FIRST = 32 * 1024 * 1024
VMEM_REST = 8 * 1024 * 1024


def steer(resid, enc_weight, enc_bias, thresholds, dec_weight, dec_bias, refusal_ids, clamp_levels):
    bf16, f32 = jnp.bfloat16, jnp.float32
    hold = lax.optimization_barrier
    lat_dev = enc_weight.shape[1]
    width = resid.shape[1]
    dp_index = lax.axis_index("dp")
    lat_index = lax.axis_index("latent")
    x_index = (lat_index // 2) % 4
    core = lat_index % 2
    own = lax.dynamic_slice_in_dim(resid, x_index * 16 + core * 8, 8, 0)

    enc_other = send(enc_weight, to_core)
    dec_other = send(dec_weight, to_core)
    columns = (dp_index * 32 + lat_index) * lat_dev + jnp.arange(lat_dev, dtype=jnp.int32)
    aux = jnp.stack([enc_bias, thresholds, clamp_targets(columns, refusal_ids, clamp_levels, thresholds)])
    aux = jnp.concatenate([aux, send(aux, to_core)], axis=1)
    weights = (aux, enc_weight, enc_other, dec_weight, dec_other)

    other = send(own, to_mirror)
    rows1 = hold(jnp.stack([own, other]))
    rows2 = jnp.stack([rows1] + [send(rows1, to_side(-k)) for k in (1, 2, 3)])
    rows2 = hold(rows2.reshape(64, width))
    near1, near3, far = (send(rows2, to_bulk(-k)) for k in (1, 3, 2))
    enc_buf, dec_buf, part0 = first_part(rows2, *weights)
    part1, part3, part2 = rest_part([near1, near3, far], aux, enc_buf, dec_buf)
    sums2, sums1, sums3 = send(part2, to_bulk(2)), send(part1, to_bulk(1)), send(part3, to_bulk(3))

    sum1 = part0 + sums1.astype(f32) + sums3.astype(f32) + sums2.astype(f32)
    sum1 = sum1.reshape(4, 16, width)
    sum2 = sum1[0]
    for k in (2, 1, 3):
        sum2 = sum2 + send(sum1[k].astype(bf16), to_side(k)).astype(f32)
    sum2 = sum2.reshape(2, 8, width)
    sum3 = sum2[0] + send(sum2[1].astype(bf16), to_mirror).astype(f32)
    mine = hold(sum3.astype(bf16))
    sum4 = mine.astype(f32) + send(mine, to_zl(1)).astype(f32)
    mine = hold(sum4.astype(bf16))
    recon = mine.astype(f32) + send(mine, to_zl(2)).astype(f32) + dec_bias

    in_sq = jnp.sum(jnp.square(own.astype(f32)), axis=1, keepdims=True)
    out_sq = jnp.sum(jnp.square(recon), axis=1, keepdims=True)
    scaled = hold((recon * jnp.sqrt((in_sq + norm_eps) / (out_sq + norm_eps))).astype(bf16))

    groups = jnp.stack([scaled] + [send(scaled, to_x(-k)) for k in (1, 2, 3)])
    groups = hold(groups)
    groups_other = send(groups, to_core)
    first = jnp.where(core == 0, groups, groups_other)
    second = jnp.where(core == 0, groups_other, groups)
    both = jnp.stack([first, second], axis=1).reshape(64, width)
    twice = jnp.concatenate([both, both], axis=0)
    return lax.dynamic_slice_in_dim(twice, (4 - x_index) % 4 * 16, 64, 0)


def solution(mesh):
    in_specs = (
        P("dp", None),
        P(None, ("dp", "latent")),
        P(("dp", "latent")),
        P(("dp", "latent")),
        P(("dp", "latent"), None),
        P(),
        P(),
        P(),
    )
    out_specs = P("dp", None)
    return jax.shard_map(steer, mesh=mesh, in_specs=in_specs, out_specs=out_specs, check_vma=False)
```
